256 devices in a mesh: prow: 32 (over y, x, core), pcol: 8 (over z).
Axes of the slice: x: 4, y: 4, z: 8, core: 2. Of those that a mesh axis runs over, the one named last changes fastest.
Arguments:
- panels: float32 [65536, 512], P('prow', 'pcol'), may hold values from -0.015625 to 0.015625
- slab: float32 [65536, 2048], P('prow', 'pcol'), may hold values from -6 to 6
Outputs:
- r_factor: float32 [512, 512], P(None, 'pcol')
- coupling: float32 [512, 2048], P(None, 'pcol')
- remainder: float32 [65536, 2048], P('prow', 'pcol')
The draws below stay inside these ranges and needn't reach their ends.
All inputs are finite; a program needn't handle non-finite values.
Results may differ from the reference program's by a relative error of at most 0.00009.
Values sent between devices are 32-bit elements; how exact they have to be, the bound alone decides.
A program may use at most 128 MiB of HBM per device.

```python
import jax
import jax.numpy as jnp
from jax import lax

PB = 256
SLAB = 2048
ROWS = 65536


def draw_panels(key, part):
    subkeys = jax.random.split(jax.random.fold_in(key, 7331), 4)
    noise_part = jnp.clip(jax.random.normal(subkeys[0], (ROWS, 2 * PB), jnp.float32), -4.0, 4.0)
    lowest = 0.4
    highest = 0.8
    common = jnp.clip(jax.random.normal(subkeys[1], (ROWS, 2), jnp.float32), -4.0, 4.0)
    loading = jax.random.uniform(subkeys[2], (2 * PB,), jnp.float32, lowest, highest)
    cross_load = jax.random.uniform(subkeys[3], (PB,), jnp.float32, 0.2, 0.5)
    columns = jnp.arange(2 * PB)
    own_factor = jnp.where(columns[None, :] < PB, common[:, 0:1], common[:, 1:2])
    cross_full = jnp.concatenate([jnp.zeros((PB,), jnp.float32), cross_load], 0)
    values = noise_part + loading[None, :] * own_factor + cross_full[None, :] * common[:, 0:1]
    row_scale = 1.0 / jnp.sqrt(jnp.float32(ROWS))
    return jnp.clip(values * row_scale, -4.0 * row_scale, 4.0 * row_scale).astype(jnp.float32)


def steps_of(rng, extent, cuts, least, largest):
    def one(dim, parts):
        steps = jax.random.uniform(jax.random.fold_in(jax.random.fold_in(rng, 6), dim), (parts,), jnp.float32, least / len(cuts), largest / len(cuts))
        return jnp.repeat(jnp.exp(steps), extent[dim] // parts).reshape((-1,) + (1,) * (len(extent) - dim - 1))

    loudness = one(*cuts[0])
    for cut in cuts[1:]:
        loudness = loudness * one(*cut)
    return loudness


def scatter_about(stream_key, shape, deviation, bound, cuts=(), dtype=jnp.bfloat16):
    array = deviation * jax.random.normal(stream_key, shape, jnp.float32)
    if cuts:
        array = array * steps_of(stream_key, shape, cuts, -0.22, 0.18)
    return jnp.clip(array, -bound, bound).astype(dtype)


def setup_inputs(seed: int = 0) -> dict:
    splits = jax.random.split(jax.random.key(seed), 3)
    panels = draw_panels(jax.random.fold_in(splits[2], 71), 0)
    slab = scatter_about(splits[1], (ROWS, SLAB), 1.0, 6.0, ((0, 32), (1, 8)), jnp.float32)
    return dict(panels=panels, slab=slab)


def tdot(left, right):
    return lax.dot_general(left.astype(jnp.float32), right.astype(jnp.float32), (((0,), (0,)), ((), ())), precision=lax.Precision.HIGHEST, preferred_element_type=jnp.float32)

def mdot(left, right):
    return jnp.dot(left.astype(jnp.float32), right.astype(jnp.float32), precision=lax.Precision.HIGHEST, preferred_element_type=jnp.float32)

def lsolve(lower, rhs):
    return jax.scipy.linalg.solve_triangular(lower, rhs, lower=True)

def usolve(lower, rhs):
    return jax.scipy.linalg.solve_triangular(lower.T, rhs, lower=False)

def reference(panels, slab):
    first = panels[:, :PB]
    second = panels[:, PB:]
    lower1 = jnp.linalg.cholesky(tdot(first, first))
    r12 = lsolve(lower1, tdot(first, second))
    top = lsolve(lower1, tdot(first, slab))
    second2 = second - mdot(first, usolve(lower1, r12))
    slab2 = slab - mdot(first, usolve(lower1, top))
    lower2 = jnp.linalg.cholesky(tdot(second2, second2))
    bottom = lsolve(lower2, tdot(second2, slab2))
    remainder = slab2 - mdot(second2, usolve(lower2, bottom))
    zeros = jnp.zeros((PB, PB), jnp.float32)
    r_factor = jnp.concatenate([jnp.concatenate([lower1.T, r12], 1), jnp.concatenate([zeros, lower2.T], 1)], 0)
    coupling = jnp.concatenate([top, bottom], 0)
    return (r_factor, coupling, remainder)
```

```python
import functools

import jax
import jax.numpy as jnp
from jax import lax
from jax.experimental import pallas as pl
from jax.experimental.pallas import tpu as pltpu
from jax.sharding import PartitionSpec as P

N = 512
BLK = 128
GRP = 8
HI = lax.Precision.HIGHEST


def factor_block(tile):
    groups = BLK // GRP
    lanes = lax.broadcasted_iota(jnp.int32, (GRP, BLK), 1)
    subs = lax.broadcasted_iota(jnp.int32, (GRP, BLK), 0)
    rows = [tile[g * GRP:(g + 1) * GRP, :] for g in range(groups)]
    upper, inverse = [], []
    for g in range(groups):
        first = g * GRP
        spread = {
            i: [jnp.broadcast_to(rows[i][:, first + k:first + k + 1], (GRP, BLK)) for k in range(GRP)]
            for i in range(g, groups)
        }
        pivot = [
            [jnp.broadcast_to(spread[g][k][r:r + 1, :], (GRP, BLK)) if k >= r else None for k in range(GRP)]
            for r in range(GRP)
        ]
        inside = (lanes >= first) & (lanes < first + GRP)
        line = [
            jnp.where(inside, jnp.where(lanes == first + r, 1.0, 0.0), jnp.broadcast_to(rows[g][r:r + 1, :], (GRP, BLK)))
            for r in range(GRP)
        ]
        recips, factors = [], []
        for j in range(GRP):
            recip = 1.0 / pivot[j][j]
            recips.append(recip)
            scaled = [pivot[j][r] * recip if r > j else None for r in range(GRP)]
            factors.append(scaled)
            for r in range(j + 1, GRP):
                for k in range(r, GRP):
                    pivot[r][k] = pivot[r][k] - scaled[r] * pivot[j][k]
                line[r] = line[r] - scaled[r] * line[j]
        back = [line[r] * recips[r] for r in range(GRP)]
        for j in range(GRP - 1, -1, -1):
            for r in range(j):
                back[r] = back[r] - factors[r][j] * back[j]
        for i in range(g + 1, groups):
            total = jnp.where(inside, 0.0, rows[i])
            for k in range(GRP):
                total = total - spread[i][k] * back[k]
            rows[i] = total
        joined = jnp.zeros((GRP, BLK), jnp.float32)
        upright = jnp.zeros((GRP, BLK), jnp.float32)
        for r in range(GRP):
            root = lax.rsqrt(pivot[r][r])
            whole = line[r]
            right = line[r]
            for k in range(r, GRP):
                right = jnp.where(lanes == first + k, pivot[r][k], right)
            joined = jnp.where(subs == r, whole * root, joined)
            upright = jnp.where(subs == r, right * root, upright)
        upper.append(jnp.where(lanes >= first + subs, upright, 0.0))
        inverse.append(jnp.where(lanes <= first + subs, joined, 0.0))
    return jnp.concatenate(upper, 0), jnp.concatenate(inverse, 0)


def hdot(left, right, dims):
    return lax.dot_general(left, right, (dims, ((), ())), precision=HI, preferred_element_type=jnp.float32)

MESH = pl.DeviceIdType.MESH
OWN = 2
TILE = (8, 128)
GT = 20
PAIRS = ((1, 3), (0, 4), (7, 5), (2, 6))


def split(x):
    high = x.astype(jnp.bfloat16)
    return high, (x - high.astype(jnp.float32)).astype(jnp.bfloat16)


def bdot(left, right, dims):
    return lax.dot_general(left, right, (dims, ((), ())), preferred_element_type=jnp.float32)


def gather_kernel(
    wt_ref, slab_ref, wall, gall, sfull,
    slab, shi, slo, spart, srecv, gpart, grecv, gz, span,
    load_sem, plus_send, plus_recv, minus_send, minus_recv,
    s_send, s_recv, a_send, a_recv, g_send, g_recv, z_send, z_recv, h_send, h_recv,
    *, rows, planes,
):
    r = lax.axis_index("prow")
    z = lax.axis_index("pcol")
    wide = wt_ref.shape[1]
    half = wide // 2
    right, left = lax.rem(z + 1, planes), lax.rem(z + planes - 1, planes)

    load = pltpu.make_async_copy(slab_ref, slab, load_sem.at[0])
    load.start()
    own = pltpu.make_async_copy(wt_ref, wall.at[OWN], load_sem.at[1])
    own.start()

    barrier = pltpu.get_barrier_semaphore()

    def greet_row(o, c):
        pl.semaphore_signal(barrier, inc=1, device_id=(lax.rem(r + o, rows), z), device_id_type=MESH)
        return c

    def greet_plane(o, c):
        pl.semaphore_signal(barrier, inc=1, device_id=(r, lax.rem(z + o, planes)), device_id_type=MESH)
        return c

    lax.fori_loop(1, planes, greet_plane, 0)
    lax.fori_loop(1, rows, greet_row, 0)
    pl.semaphore_wait(barrier, rows - 1 + planes - 1)

    def piece(h):
        return pl.ds(h * half, half)

    plus_slot = [OWN, 1, 0, 7, 6]
    minus_slot = [OWN, 3, 4, 5, 6]

    def hop(step, h, plus):
        slots = plus_slot if plus else minus_slot
        src = wt_ref if step == 1 else wall.at[slots[step - 1]]
        send, recv = (plus_send, plus_recv) if plus else (minus_send, minus_recv)
        n = 2 * (step - 1) + h
        return pltpu.make_async_remote_copy(
            src_ref=src.at[:, piece(h)],
            dst_ref=wall.at[slots[step], :, piece(h)],
            send_sem=send.at[n],
            recv_sem=recv.at[n],
            device_id=(r, right if plus else left),
            device_id_type=MESH,
        )

    hops = {}
    for step in (1, 2, 3):
        for h in (0, 1):
            for plus in (True, False):
                hops[step, h, plus] = hop(step, h, plus)
    hops[4, 0, True] = hop(4, 0, True)
    hops[4, 1, False] = hop(4, 1, False)

    def forward(step):
        for h in (0, 1):
            for plus in (True, False):
                hops[step, h, plus].wait_recv()
                if (step + 1, h, plus) in hops:
                    hops[step + 1, h, plus].start()

    for h in (0, 1):
        for plus in (True, False):
            hops[1, h, plus].start()

    def tiles_out(acc, g, base):
        for t in range(acc.shape[0] // 8 * 2):
            spart[g, base + t] = acc[8 * (t // 2):8 * (t // 2) + 8, 128 * (t % 2):128 * (t % 2) + 128]

    def product(slots):
        parts = [split(wall[k]) for k in slots]
        highs = [p[0] for p in parts]
        n = 64 * len(slots)
        both = bdot(jnp.concatenate(highs + [p[1] for p in parts], 0), shi[...], ((1,), (0,)))
        cross = bdot(jnp.concatenate(highs, 0), slo[...], ((1,), (0,)))
        return both[:n] + both[n:] + cross

    def scatter(part, recv_buf, count, send, recv):
        recv_at = recv_buf.at[r]

        def body(t, c):
            @pl.when(t != r)
            def _():
                pltpu.make_async_remote_copy(
                    src_ref=part.at[t], dst_ref=recv_at, send_sem=send, recv_sem=recv,
                    device_id=(t, z), device_id_type=MESH,
                ).start()
            return c

        lax.fori_loop(0, count, body, 0)

    def drain(ref, sem):
        pltpu.make_async_copy(ref, ref, sem).wait()

    def s_scatter(g):
        srecv[g, r] = spart[g, r]
        scatter(spart.at[g], srecv.at[g], rows, s_send.at[g], s_recv.at[g])

    def s_gather(g):
        drain(srecv.at[g, pl.ds(0, rows - 1)], s_recv.at[g])
        total = srecv[g, 0]
        for q in range(1, rows):
            total = total + srecv[g, q]
        sfull[g, r] = total

        def body(o, c):
            pltpu.make_async_remote_copy(
                src_ref=sfull.at[g, r], dst_ref=sfull.at[g, r], send_sem=a_send.at[g], recv_sem=a_recv.at[g],
                device_id=(lax.rem(r + o, rows), z), device_id_type=MESH,
            ).start()
            return c

        lax.fori_loop(1, rows, body, 0)

    def gram_scatter():
        window = [split(wall[k]) for k in range(5)]
        vhi, vlo = window[0]
        first = bdot(jnp.concatenate([vhi, vlo], 0), jnp.concatenate([w[0] for w in window], 0), ((1,), (1,)))
        second = bdot(vhi, jnp.concatenate([w[1] for w in window], 0), ((1,), (1,)))
        acc = first[:64] + first[64:] + second
        packed = [acc[:, :128], acc[:, 128:256], jnp.concatenate([acc[:32, 256:], acc[32:, 256:]], 1)]
        n = 0
        for p in packed:
            for t in range(p.shape[0] // 8):
                gpart[n] = p[8 * t:8 * t + 8]
                n += 1

        @pl.when(r < GT)
        def _():
            grecv[r] = gpart[r]

        scatter(gpart, grecv, GT, g_send.at[0], g_recv.at[0])

    def gram_across():
        @pl.when(r < GT)
        def _():
            drain(grecv.at[pl.ds(0, rows - 1)], g_recv.at[0])
            total = grecv[0]
            for q in range(1, rows):
                total = total + grecv[q]
            gz[z] = total

            def body(o, c):
                pltpu.make_async_remote_copy(
                    src_ref=gz.at[z], dst_ref=gz.at[z], send_sem=z_send.at[0], recv_sem=z_recv.at[0],
                    device_id=(r, lax.rem(z + o, planes)), device_id_type=MESH,
                ).start()
                return c

            lax.fori_loop(1, planes, body, 0)

    def gram_gather():
        @pl.when(r < GT)
        def _():
            drain(gz.at[pl.ds(0, planes - 1)], z_recv.at[0])
            gall[r] = gz[...]

            def body(o, c):
                pltpu.make_async_remote_copy(
                    src_ref=gz, dst_ref=gall.at[r], send_sem=h_send.at[0], recv_sem=h_recv.at[0],
                    device_id=(lax.rem(r + o, rows), z), device_id_type=MESH,
                ).start()
                return c

            lax.fori_loop(1, rows, body, 0)

    load.wait()
    own.wait()
    high, low = split(slab[...])
    shi[...] = high
    slo[...] = low
    tiles_out(product((OWN,)), 3, 0)

    forward(1)
    tiles_out(product(PAIRS[0]), 0, 0)
    s_scatter(0)
    forward(2)
    gram_scatter()
    tiles_out(product(PAIRS[1]), 1, 0)
    s_scatter(1)
    gram_across()
    s_gather(0)
    forward(3)
    gram_gather()
    tiles_out(product(PAIRS[2]), 2, 0)
    s_scatter(2)
    s_gather(1)
    hops[4, 0, True].wait_recv()
    hops[4, 1, False].wait_recv()
    tiles_out(product((6,)), 3, 16)
    s_scatter(3)
    s_gather(2)
    s_gather(3)

    for copy in hops.values():
        copy.wait_send()
    for g in range(4):
        drain(spart.at[g, pl.ds(0, rows - 1)], s_send.at[g])
        drain(sfull.at[g, pl.ds(0, rows - 1)], a_send.at[g])
        drain(sfull.at[g, pl.ds(0, rows - 1)], a_recv.at[g])

    @pl.when(r < GT)
    def _():
        drain(gpart.at[pl.ds(0, GT - 1)], g_send.at[0])
        drain(gz.at[pl.ds(0, planes - 1)], z_send.at[0])
        drain(span, h_send.at[0])
        drain(gall.at[pl.ds(0, GT - 1)], h_recv.at[0])

    @pl.when(r >= GT)
    def _():
        drain(gpart.at[pl.ds(0, GT)], g_send.at[0])
        drain(gall, h_recv.at[0])


def gather_reduce(wt, slab, rows, planes):
    depth, width = slab.shape
    any_ = pl.BlockSpec(memory_space=pl.ANY)
    vmem = pl.BlockSpec(memory_space=pltpu.VMEM)
    f32 = jnp.float32
    dma = pltpu.SemaphoreType.DMA
    return pl.pallas_call(
        functools.partial(gather_kernel, rows=rows, planes=planes),
        out_shape=(
            jax.ShapeDtypeStruct((planes, wt.shape[0], depth), f32),
            jax.ShapeDtypeStruct((GT, planes) + TILE, f32),
            jax.ShapeDtypeStruct((4, rows) + TILE, f32),
        ),
        in_specs=[any_] * 2,
        out_specs=(vmem,) * 3,
        scratch_shapes=[
            pltpu.VMEM((depth, width), f32),
            pltpu.VMEM((depth, width), jnp.bfloat16),
            pltpu.VMEM((depth, width), jnp.bfloat16),
            pltpu.VMEM((4, rows) + TILE, f32),
            pltpu.VMEM((4, rows) + TILE, f32),
            pltpu.VMEM((GT,) + TILE, f32),
            pltpu.VMEM((rows,) + TILE, f32),
            pltpu.VMEM((planes,) + TILE, f32),
            pltpu.VMEM((rows - 1, planes) + TILE, f32),
            dma((2,)), dma((8,)), dma((8,)), dma((8,)), dma((8,)),
            dma((4,)), dma((4,)), dma((4,)), dma((4,)),
            dma((1,)), dma((1,)), dma((1,)), dma((1,)), dma((1,)), dma((1,)),
        ],
        compiler_params=pltpu.CompilerParams(
            collective_id=0, has_side_effects=True, vmem_limit_bytes=60 << 20
        ),
    )(wt, slab)


def hdot(left, right, dims):
    return lax.dot_general(left, right, (dims, ((), ())), precision=HI, preferred_element_type=jnp.float32)


def assemble(gall, work):
    def part(i, d):
        p = (i + 2) % 8
        first = 8 * (d // 2)
        count = 4 if d == 4 else 8
        both = jnp.concatenate([gall[first + t, p] for t in range(count)], 0)
        if d == 4:
            return jnp.concatenate([both[:, :64], both[:, 64:]], 0)
        return both[:, 64 * (d % 2):64 * (d % 2) + 64]

    def block(a, b):
        if a > b:
            return block(b, a).T
        if b - a <= 4:
            return part(a, b - a)
        return part(b, 8 - (b - a)).T

    for a in range(8):
        for pair in range(a // 2, 4):
            work[64 * a:64 * a + 64, 128 * pair:128 * pair + 128] = jnp.concatenate(
                [block(a, 2 * pair), block(a, 2 * pair + 1)], 1
            )


def chol_kernel(gall, sfull, rt_ref, coupling_ref, xrel_ref, work, upper_ref, inv, x_ref, turned):
    z = lax.axis_index("pcol")
    width = coupling_ref.shape[1]
    work[...] = jnp.zeros_like(work)
    assemble(gall, work)
    for g in range(4):
        for t in range(32):
            base = 64 * lax.rem(z + 6 + PAIRS[g][t // 16], 8) + 8 * ((t // 2) % 8)
            work[pl.ds(pl.multiple_of(base, 8), 8), N + 128 * (t % 2):N + 128 * (t % 2) + 128] = sfull[g, t]
    columns = lax.broadcasted_iota(jnp.int32, (BLK, N + width), 1)

    def body(k, carry):
        start = pl.multiple_of(k * BLK, BLK)
        upper, inverse = factor_block(work[pl.ds(start, BLK), pl.ds(start, BLK)])
        inv[k] = inverse
        across = hdot(inverse, work[pl.ds(start, BLK), :], ((1,), (0,)))
        across = jnp.where(columns >= start + BLK, across, 0.0)
        upper_ref[pl.ds(start, BLK), :] = across[:, :N]
        upper_ref[pl.ds(start, BLK), pl.ds(start, BLK)] = upper
        coupling_ref[pl.ds(start, BLK), :] = across[:, N:]
        work[...] -= hdot(across[:, :N], across, ((0,), (0,)))
        return carry

    lax.fori_loop(0, N // BLK, body, 0)
    for k in range(N // BLK - 1, -1, -1):
        rhs = coupling_ref[k * BLK:(k + 1) * BLK, :]
        if k < N // BLK - 1:
            rhs = rhs - hdot(upper_ref[k * BLK:(k + 1) * BLK, (k + 1) * BLK:], x_ref[(k + 1) * BLK:, :], ((1,), (0,)))
        x_ref[k * BLK:(k + 1) * BLK, :] = hdot(inv[k], rhs, ((0,), (0,)))
    for b in range(8):
        slot = lax.rem(b + 10 - z, 8)
        xrel_ref[pl.ds(pl.multiple_of(64 * slot, 64), 64), :] = x_ref[64 * b:64 * b + 64, :]
    first = pl.multiple_of(lax.div(z, 2) * 128, 128)
    turned[...] = upper_ref[:, pl.ds(first, 128)].T
    rt_ref[...] = turned[pl.ds(pl.multiple_of(64 * lax.rem(z, 2), 64), 64), :]


def chol_solve(gall, sfull, width):
    vmem = pl.BlockSpec(memory_space=pltpu.VMEM)
    f32 = jnp.float32
    return pl.pallas_call(
        chol_kernel,
        out_shape=(
            jax.ShapeDtypeStruct((64, N), f32),
            jax.ShapeDtypeStruct((N, width), f32),
            jax.ShapeDtypeStruct((N, width), f32),
        ),
        in_specs=[vmem] * 2,
        out_specs=(vmem,) * 3,
        scratch_shapes=[
            pltpu.VMEM((N, N + width), f32),
            pltpu.VMEM((N, N), f32),
            pltpu.VMEM((N // BLK, BLK, BLK), f32),
            pltpu.VMEM((N, width), f32),
            pltpu.VMEM((BLK, N), f32),
        ],
        compiler_params=pltpu.CompilerParams(vmem_limit_bytes=24 << 20),
    )(gall, sfull)


def remainder_kernel(wall, x_ref, slab_ref, out_ref, xhi, xlo):
    @pl.when(pl.program_id(0) == 0)
    def _():
        high, low = split(x_ref[...])
        xhi[...] = high
        xlo[...] = low

    whi, wlo = split(wall[...].reshape(N, wall.shape[2]))
    dims = ((0,), (0,))
    moved = bdot(whi, xhi[...], dims) + bdot(wlo, xhi[...], dims) + bdot(whi, xlo[...], dims)
    out_ref[...] = slab_ref[...] - moved


def remove(wall, xrel, slab):
    rows, width = slab.shape
    tile = 512
    return pl.pallas_call(
        remainder_kernel,
        out_shape=jax.ShapeDtypeStruct((rows, width), jnp.float32),
        grid=(rows // tile,),
        in_specs=[
            pl.BlockSpec((wall.shape[0], wall.shape[1], tile), lambda i: (0, 0, i)),
            pl.BlockSpec((N, width), lambda i: (0, 0)),
            pl.BlockSpec((tile, width), lambda i: (i, 0)),
        ],
        out_specs=pl.BlockSpec((tile, width), lambda i: (i, 0)),
        scratch_shapes=[pltpu.VMEM((N, width), jnp.bfloat16), pltpu.VMEM((N, width), jnp.bfloat16)],
        compiler_params=pltpu.CompilerParams(vmem_limit_bytes=24 << 20),
    )(wall, xrel, slab)


def per_device(rows, planes, panels, slab):
    wall, gall, sfull = gather_reduce(panels.T, slab, rows, planes)
    turned, coupling, xrel = chol_solve(gall, sfull, slab.shape[1])
    return (turned.T, coupling, remove(wall, xrel, slab))


def solution(mesh):
    placed = (P("prow", "pcol"), P("prow", "pcol"))
    return jax.shard_map(
        functools.partial(per_device, mesh.shape["prow"], mesh.shape["pcol"]),
        mesh=mesh,
        in_specs=placed,
        out_specs=(P(None, "pcol"), P(None, "pcol"), P("prow", "pcol")),
        check_vma=False,
    )
```

```python
import functools

import jax
import jax.numpy as jnp
from jax import lax
from jax.experimental import pallas as pl
from jax.experimental.pallas import tpu as pltpu
from jax.sharding import PartitionSpec as P

MESH = pl.DeviceIdType.MESH
N = 512
BLK = 128
GRP = 8
SUB = 32
HI = lax.Precision.HIGHEST
OWN = 2
TILE = (8, 128)
GT = 20
G0 = 12
PAIRS = ((1, 3), (0, 4), (7, 5), (2, 6))


def split(x):
    high = x.astype(jnp.bfloat16)
    return high, (x - high.astype(jnp.float32)).astype(jnp.bfloat16)


def bdot(left, right, dims):
    return lax.dot_general(left, right, (dims, ((), ())), preferred_element_type=jnp.float32)


def dot3(left, right, dims):
    lhi, llo = split(left)
    rhi, rlo = split(right)
    return bdot(lhi, rhi, dims) + (bdot(lhi, rlo, dims) + bdot(llo, rhi, dims))


def hdot(left, right, dims):
    return lax.dot_general(left, right, (dims, ((), ())), precision=HI, preferred_element_type=jnp.float32)


def factor_block(tile):
    groups = BLK // GRP
    near = SUB // GRP
    lanes = lax.broadcasted_iota(jnp.int32, (GRP, BLK), 1)
    subs = lax.broadcasted_iota(jnp.int32, (GRP, BLK), 0)
    rows = [tile[g * GRP:(g + 1) * GRP, :] for g in range(groups)]
    upper, inverse, scaled_rows, masked_rows = [], [], [], []
    for g in range(groups):
        first = g * GRP
        last = (g // near + 1) * near
        spread = {
            i: [jnp.broadcast_to(rows[i][:, first + k:first + k + 1], (GRP, BLK)) for k in range(GRP)]
            for i in range(g, last)
        }
        pivot = [
            [jnp.broadcast_to(spread[g][k][r:r + 1, :], (GRP, BLK)) if k >= r else None for k in range(GRP)]
            for r in range(GRP)
        ]
        inside = (lanes >= first) & (lanes < first + GRP)
        line = [
            jnp.where(inside, jnp.where(lanes == first + r, 1.0, 0.0), jnp.broadcast_to(rows[g][r:r + 1, :], (GRP, BLK)))
            for r in range(GRP)
        ]
        recips, factors = [], []
        for j in range(GRP):
            recip = 1.0 / pivot[j][j]
            recips.append(recip)
            scaled = [pivot[j][r] * recip if r > j else None for r in range(GRP)]
            factors.append(scaled)
            for r in range(j + 1, GRP):
                for k in range(r, GRP):
                    pivot[r][k] = pivot[r][k] - scaled[r] * pivot[j][k]
                line[r] = line[r] - scaled[r] * line[j]
        if g + 1 < last:
            back = [line[r] * recips[r] for r in range(GRP)]
            for j in range(GRP - 1, -1, -1):
                for r in range(j):
                    back[r] = back[r] - factors[r][j] * back[j]
            for i in range(g + 1, last):
                total = jnp.where(inside, 0.0, rows[i])
                for k in range(GRP):
                    total = total - spread[i][k] * back[k]
                rows[i] = total
        joined = jnp.zeros((GRP, BLK), jnp.float32)
        upright = jnp.zeros((GRP, BLK), jnp.float32)
        for r in range(GRP):
            root = lax.rsqrt(pivot[r][r])
            right = line[r]
            for k in range(r, GRP):
                right = jnp.where(lanes == first + k, pivot[r][k], right)
            joined = jnp.where(subs == r, line[r] * root, joined)
            upright = jnp.where(subs == r, right * root, upright)
        scaled_rows.append(joined)
        masked_rows.append(jnp.where((lanes >= first + GRP) & (lanes < last * GRP), 0.0, joined))
        upper.append(jnp.where(lanes >= first + subs, upright, 0.0))
        inverse.append(jnp.where(lanes <= first + subs, joined, 0.0))
        if g + 1 == last and last < groups:
            begin = (last - near) * GRP
            done = jnp.concatenate(scaled_rows[last - near:last], 0)
            kept = jnp.concatenate(masked_rows[last - near:last], 0)
            change = hdot(done, kept, ((0,), (0,)))
            cleared = (lanes >= begin) & (lanes < last * GRP)
            for i in range(last, groups):
                rows[i] = jnp.where(cleared, 0.0, rows[i]) - change[i * GRP:(i + 1) * GRP, :]
    return jnp.concatenate(upper, 0), jnp.concatenate(inverse, 0)


def carry_rhs(b, inv, upper_ref, work, coupling_ref):
    low, high = b * BLK, (b + 1) * BLK
    part = hdot(inv[b], work[low:high, N:], ((1,), (0,)))
    coupling_ref[low:high, :] = part
    if high < N:
        work[high:, N:] -= dot3(upper_ref[low:high, high:], part, ((0,), (0,)))


def factor_all(work, inv, upper_ref, after):
    blocks = N // BLK

    def body(k, carry):
        start = pl.multiple_of(k * BLK, BLK)
        upper, inverse = factor_block(work[pl.ds(start, BLK), pl.ds(start, BLK)])
        inv[k] = inverse
        upper_ref[pl.ds(start, BLK), pl.ds(start, BLK)] = upper
        for b in range(blocks):
            @pl.when(k == b)
            def _():
                low, high = b * BLK, (b + 1) * BLK
                dims = ((0,), (0,))
                if high < N:
                    across = hdot(inv[b], work[low:high, high:N], ((1,), (0,)))
                    upper_ref[low:high, high:] = across
                    for c in range(b + 1, blocks):
                        top = c * BLK - high
                        work[c * BLK:(c + 1) * BLK, c * BLK:N] -= dot3(across[:, top:top + BLK], across[:, top:], dims)
                after(b)
        return carry

    lax.fori_loop(0, blocks, body, 0)


def back_solve(inv, upper_ref, coupling_ref, x_ref):
    blocks = N // BLK
    for k in range(blocks - 1, -1, -1):
        rhs = coupling_ref[k * BLK:(k + 1) * BLK, :]
        if k < blocks - 1:
            rhs = rhs - dot3(upper_ref[k * BLK:(k + 1) * BLK, (k + 1) * BLK:], x_ref[(k + 1) * BLK:, :], ((1,), (0,)))
        x_ref[k * BLK:(k + 1) * BLK, :] = dot3(inv[k], rhs, ((0,), (0,)))


def assemble(gall, work):
    def part(i, d):
        p = (i + 2) % 8
        first = 8 * (d // 2)
        count = 4 if d == 4 else 8
        both = jnp.concatenate([gall[first + t, p] for t in range(count)], 0)
        if d == 4:
            return jnp.concatenate([both[:, :64], both[:, 64:]], 0)
        return both[:, 64 * (d % 2):64 * (d % 2) + 64]

    def block(a, b):
        if a > b:
            return block(b, a).T
        if b - a <= 4:
            return part(a, b - a)
        return part(b, 8 - (b - a)).T

    for a in range(8):
        for pair in range(a // 2, 4):
            work[64 * a:64 * a + 64, 128 * pair:128 * pair + 128] = jnp.concatenate(
                [block(a, 2 * pair), block(a, 2 * pair + 1)], 1
            )


def gram_owner(q):
    if q < G0:
        return 8 * (q // 3) + (0, 4, 6)[q % 3]
    return 8 * ((q - G0) // 2) + (1, 3)[(q - G0) % 2]


def main_kernel(
    wt_ref, slab_ref, wall, xrel_ref, coupling_ref, rt_ref,
    gall, sfull, slab, shi, slo, spart, srecv, gpart, grecv, gz, span, work, upper_ref, inv, x_ref, turned,
    load_sem, plus_send, plus_recv, minus_send, minus_recv,
    s_send, s_recv, a_send, a_recv, g_send, g_recv, z_send, z_recv, h_send, h_recv, p_send, p_recv,
    *, rows, planes,
):
    r = lax.axis_index("prow")
    z = lax.axis_index("pcol")
    wide = wt_ref.shape[1]
    half = wide // 2
    right, left = lax.rem(z + 1, planes), lax.rem(z + planes - 1, planes)
    core, spot, line = lax.rem(r, 2), lax.rem(r, 8), lax.div(r, 8)
    reducer = ((core == 0) & (spot != 2)) | ((core == 1) & (spot < 4))
    near = lax.div(spot, 2)
    place = jnp.where(core == 0, 3 * line + near - jnp.minimum(near, 1), G0 + 2 * line + near)

    load = pltpu.make_async_copy(slab_ref, slab, load_sem.at[0])
    load.start()
    own = pltpu.make_async_copy(wt_ref, wall.at[OWN], load_sem.at[1])
    own.start()

    barrier = pltpu.get_barrier_semaphore()

    def greet_row(o, c):
        pl.semaphore_signal(barrier, inc=1, device_id=(lax.rem(r + o, rows), z), device_id_type=MESH)
        return c

    def greet_plane(o, c):
        pl.semaphore_signal(barrier, inc=1, device_id=(r, lax.rem(z + o, planes)), device_id_type=MESH)
        return c

    lax.fori_loop(1, planes, greet_plane, 0)
    lax.fori_loop(1, rows, greet_row, 0)
    pl.semaphore_wait(barrier, rows - 1 + planes - 1)

    def piece(h):
        return pl.ds(h * half, half)

    plus_slot = [OWN, 1, 0, 7, 6]
    minus_slot = [OWN, 3, 4, 5, 6]

    def hop(step, h, plus):
        slots = plus_slot if plus else minus_slot
        src = wt_ref if step == 1 else wall.at[slots[step - 1]]
        send, recv = (plus_send, plus_recv) if plus else (minus_send, minus_recv)
        n = 2 * (step - 1) + h
        return pltpu.make_async_remote_copy(
            src_ref=src.at[:, piece(h)],
            dst_ref=wall.at[slots[step], :, piece(h)],
            send_sem=send.at[n],
            recv_sem=recv.at[n],
            device_id=(r, right if plus else left),
            device_id_type=MESH,
        )

    hops = {}
    for step in (1, 2, 3):
        for h in (0, 1):
            for plus in (True, False):
                hops[step, h, plus] = hop(step, h, plus)
    hops[4, 0, True] = hop(4, 0, True)
    hops[4, 1, False] = hop(4, 1, False)

    def forward(step, parts=(0, 1)):
        for h in parts:
            for plus in (True, False):
                hops[step, h, plus].wait_recv()
                if (step + 1, h, plus) in hops:
                    hops[step + 1, h, plus].start()

    for h in (0, 1):
        for plus in (True, False):
            hops[1, h, plus].start()

    def tiles_out(acc, g, base):
        for t in range(acc.shape[0] // 8 * 2):
            spart[g, base + t] = acc[8 * (t // 2):8 * (t // 2) + 8, 128 * (t % 2):128 * (t % 2) + 128]

    def product(slots):
        parts = [split(wall[k]) for k in slots]
        highs = [p[0] for p in parts]
        n = 64 * len(slots)
        both = bdot(jnp.concatenate(highs + [p[1] for p in parts], 0), shi[...], ((1,), (0,)))
        cross = bdot(jnp.concatenate(highs, 0), slo[...], ((1,), (0,)))
        return both[:n] + both[n:] + cross

    def scatter(part, recv_buf, count, send, recv):
        recv_at = recv_buf.at[r]

        def body(t, c):
            @pl.when(t != r)
            def _():
                pltpu.make_async_remote_copy(
                    src_ref=part.at[t], dst_ref=recv_at, send_sem=send, recv_sem=recv,
                    device_id=(t, z), device_id_type=MESH,
                ).start()
            return c

        lax.fori_loop(0, count, body, 0)

    def drain(ref, sem):
        pltpu.make_async_copy(ref, ref, sem).wait()

    def s_scatter(g):
        srecv[g, r] = spart[g, r]
        scatter(spart.at[g], srecv.at[g], rows, s_send.at[g], s_recv.at[g])

    def s_gather(g):
        drain(srecv.at[g, pl.ds(0, rows - 1)], s_recv.at[g])
        total = srecv[g, 0]
        for q in range(1, rows):
            total = total + srecv[g, q]
        sfull[g, r] = total

        def body(o, c):
            pltpu.make_async_remote_copy(
                src_ref=sfull.at[g, r], dst_ref=sfull.at[g, r], send_sem=a_send.at[g], recv_sem=a_recv.at[g],
                device_id=(lax.rem(r + o, rows), z), device_id_type=MESH,
            ).start()
            return c

        lax.fori_loop(1, rows, body, 0)

    def gram_scatter():
        window = [split(wall[k]) for k in range(5)]
        vhi, vlo = window[0]
        first = bdot(jnp.concatenate([vhi, vlo], 0), jnp.concatenate([w[0] for w in window], 0), ((1,), (1,)))
        second = bdot(vhi, jnp.concatenate([w[1] for w in window], 0), ((1,), (1,)))
        acc = first[:64] + first[64:] + second
        packed = [acc[:, :128], acc[:, 128:256], jnp.concatenate([acc[:32, 256:], acc[32:, 256:]], 1)]
        n = 0
        for p in packed:
            for t in range(p.shape[0] // 8):
                gpart[n] = p[8 * t:8 * t + 8]
                n += 1

        @pl.when(reducer)
        def _():
            grecv[r] = gpart[place]

        for q in range(GT):
            @pl.when(r != gram_owner(q))
            def _():
                pltpu.make_async_remote_copy(
                    src_ref=gpart.at[q], dst_ref=grecv.at[r], send_sem=g_send.at[0], recv_sem=g_recv.at[0],
                    device_id=(gram_owner(q), z), device_id_type=MESH,
                ).start()

    def gram_across():
        @pl.when(reducer)
        def _():
            drain(grecv.at[pl.ds(0, rows - 1)], g_recv.at[0])
            total = grecv[0]
            for q in range(1, rows):
                total = total + grecv[q]
            gz[z] = total

            def body(o, c):
                pltpu.make_async_remote_copy(
                    src_ref=gz.at[z], dst_ref=gz.at[z], send_sem=z_send.at[0], recv_sem=z_recv.at[0],
                    device_id=(r, lax.rem(z + o, planes)), device_id_type=MESH,
                ).start()
                return c

            lax.fori_loop(1, planes, body, 0)

    def gram_gather():
        @pl.when(reducer)
        def _():
            drain(gz.at[pl.ds(0, planes - 1)], z_recv.at[0])
            gall[place] = gz[...]

            def body(o, c):
                pltpu.make_async_remote_copy(
                    src_ref=gz, dst_ref=gall.at[place], send_sem=h_send.at[0], recv_sem=h_recv.at[0],
                    device_id=(lax.rem(r + 2 * o, rows), z), device_id_type=MESH,
                ).start()
                return c

            lax.fori_loop(1, rows // 2, body, 0)

    parts_of = (gall.at[pl.ds(0, G0)], gall.at[pl.ds(G0, GT - G0)])

    def pair_copy(c):
        return pltpu.make_async_remote_copy(
            src_ref=parts_of[c], dst_ref=parts_of[c], send_sem=p_send.at[0], recv_sem=p_recv.at[0],
            device_id=(r + 1 - 2 * c, z), device_id_type=MESH,
        )

    def gram_pair():
        for c in (0, 1):
            count = (G0, GT - G0)[c]

            @pl.when((core == c) & reducer)
            def _():
                drain(gall.at[pl.ds(0, count - 1)], h_recv.at[0])

            @pl.when((core == c) & jnp.logical_not(reducer))
            def _():
                drain(gall.at[pl.ds(0, count)], h_recv.at[0])

            @pl.when(core == c)
            def _():
                pair_copy(c).start()

    def gram_wait():
        for c in (0, 1):
            @pl.when(core == c)
            def _():
                drain(parts_of[1 - c], p_recv.at[0])

    def s_place():
        for g in range(4):
            drain(sfull.at[g, pl.ds(0, rows - 1)], a_recv.at[g])
        for g in range(4):
            for t in range(32):
                base = 64 * lax.rem(z + 6 + PAIRS[g][t // 16], 8) + 8 * ((t // 2) % 8)
                work[pl.ds(pl.multiple_of(base, 8), 8), N + 128 * (t % 2):N + 128 * (t % 2) + 128] = sfull[g, t]

    def after(b):
        if b == 0:
            hops[4, 0, True].wait_recv()
            hops[4, 1, False].wait_recv()
            tiles_out(product((6,)), 3, 16)
            s_scatter(3)
            s_gather(2)
        if b == 1:
            s_gather(3)
        if b == 2:
            s_place()
            for c in range(3):
                carry_rhs(c, inv, upper_ref, work, coupling_ref)
        if b == 3:
            carry_rhs(3, inv, upper_ref, work, coupling_ref)

    load.wait()
    own.wait()
    high, low = split(slab[...])
    shi[...] = high
    slo[...] = low
    tiles_out(product((OWN,)), 3, 0)

    forward(1)
    tiles_out(product(PAIRS[0]), 0, 0)
    s_scatter(0)
    forward(2)
    gram_scatter()
    tiles_out(product(PAIRS[1]), 1, 0)
    gram_across()
    s_scatter(1)
    s_gather(0)
    forward(3, (0,))
    gram_gather()
    forward(3, (1,))
    tiles_out(product(PAIRS[2]), 2, 0)
    gram_pair()
    s_scatter(2)
    s_gather(1)
    upper_ref[...] = jnp.zeros_like(upper_ref)
    gram_wait()
    assemble(gall, work)
    factor_all(work, inv, upper_ref, after)
    back_solve(inv, upper_ref, coupling_ref, x_ref)
    for b in range(8):
        slot = lax.rem(b + 10 - z, 8)
        xrel_ref[pl.ds(pl.multiple_of(64 * slot, 64), 64), :] = x_ref[64 * b:64 * b + 64, :]
    first = pl.multiple_of(lax.div(z, 2) * 128, 128)
    turned[...] = upper_ref[:, pl.ds(first, 128)].T
    rt_ref[...] = turned[pl.ds(pl.multiple_of(64 * lax.rem(z, 2), 64), 64), :]

    for copy in hops.values():
        copy.wait_send()
    for g in range(4):
        drain(spart.at[g, pl.ds(0, rows - 1)], s_send.at[g])
        drain(sfull.at[g, pl.ds(0, rows - 1)], a_send.at[g])

    @pl.when(reducer)
    def _():
        drain(gpart.at[pl.ds(0, GT - 1)], g_send.at[0])
        drain(gz.at[pl.ds(0, planes - 1)], z_send.at[0])
        drain(span, h_send.at[0])

    @pl.when(jnp.logical_not(reducer))
    def _():
        drain(gpart, g_send.at[0])

    for c in (0, 1):
        @pl.when(core == c)
        def _():
            drain(parts_of[c], p_send.at[0])


def window(wt, slab, rows, planes):
    depth, width = slab.shape
    hbm = pl.BlockSpec(memory_space=pltpu.HBM)
    vmem = pl.BlockSpec(memory_space=pltpu.VMEM)
    f32 = jnp.float32
    dma = pltpu.SemaphoreType.DMA
    return pl.pallas_call(
        functools.partial(main_kernel, rows=rows, planes=planes),
        out_shape=(
            jax.ShapeDtypeStruct((planes, wt.shape[0], depth), f32),
            jax.ShapeDtypeStruct((N, width), f32),
            jax.ShapeDtypeStruct((N, width), f32),
            jax.ShapeDtypeStruct((64, N), f32),
        ),
        in_specs=[hbm] * 2,
        out_specs=(vmem,) * 4,
        scratch_shapes=[
            pltpu.VMEM((GT, planes) + TILE, f32),
            pltpu.VMEM((4, rows) + TILE, f32),
            pltpu.VMEM((depth, width), f32),
            pltpu.VMEM((depth, width), jnp.bfloat16),
            pltpu.VMEM((depth, width), jnp.bfloat16),
            pltpu.VMEM((4, rows) + TILE, f32),
            pltpu.VMEM((4, rows) + TILE, f32),
            pltpu.VMEM((GT,) + TILE, f32),
            pltpu.VMEM((rows,) + TILE, f32),
            pltpu.VMEM((planes,) + TILE, f32),
            pltpu.VMEM((rows // 2 - 1, planes) + TILE, f32),
            pltpu.VMEM((N, N + width), f32),
            pltpu.VMEM((N, N), f32),
            pltpu.VMEM((N // BLK, BLK, BLK), f32),
            pltpu.VMEM((N, width), f32),
            pltpu.VMEM((BLK, N), f32),
            dma((2,)), dma((8,)), dma((8,)), dma((8,)), dma((8,)),
            dma((4,)), dma((4,)), dma((4,)), dma((4,)),
            dma((1,)), dma((1,)), dma((1,)), dma((1,)), dma((1,)), dma((1,)), dma((1,)), dma((1,)),
        ],
        compiler_params=pltpu.CompilerParams(
            collective_id=0, has_side_effects=True, vmem_limit_bytes=40 << 20
        ),
    )(wt, slab)


def remainder_kernel(wall, x_ref, slab_ref, coupling_in, rt_in, out_ref, coupling_out, rt_out, xhi, xlo):
    coupling_out[...] = coupling_in[...]
    rt_out[...] = rt_in[...]

    @pl.when(pl.program_id(0) == 0)
    def _():
        high, low = split(x_ref[...])
        xhi[...] = high
        xlo[...] = low

    whi, wlo = split(wall[...].reshape(N, wall.shape[2]))
    dims = ((0,), (0,))
    moved = bdot(whi, xhi[...], dims) + bdot(wlo, xhi[...], dims) + bdot(whi, xlo[...], dims)
    out_ref[...] = slab_ref[...] - moved


def remove(wall, xrel, slab, coupling, turned):
    rows, width = slab.shape
    tile = 512
    steps = rows // tile
    f32 = jnp.float32
    slab_spec = pl.BlockSpec((tile, width), lambda i: (i, 0))
    coupling_spec = pl.BlockSpec((N // steps, width), lambda i: (i, 0))
    turned_spec = pl.BlockSpec((turned.shape[0] // steps, N), lambda i: (i, 0))
    return pl.pallas_call(
        remainder_kernel,
        out_shape=(
            jax.ShapeDtypeStruct((rows, width), f32),
            jax.ShapeDtypeStruct(coupling.shape, f32),
            jax.ShapeDtypeStruct(turned.shape, f32),
        ),
        grid=(steps,),
        in_specs=[
            pl.BlockSpec((wall.shape[0], wall.shape[1], tile), lambda i: (0, 0, i)),
            pl.BlockSpec((N, width), lambda i: (0, 0)),
            slab_spec, coupling_spec, turned_spec,
        ],
        out_specs=(slab_spec, coupling_spec, turned_spec),
        scratch_shapes=[pltpu.VMEM((N, width), jnp.bfloat16), pltpu.VMEM((N, width), jnp.bfloat16)],
        compiler_params=pltpu.CompilerParams(vmem_limit_bytes=24 << 20),
    )(wall, xrel, slab, coupling, turned)


def per_device(rows, planes, panels, slab):
    wall, xrel, coupling, turned = window(pltpu.with_memory_space_constraint(panels.T, pltpu.HBM), pltpu.with_memory_space_constraint(slab, pltpu.HBM), rows, planes)
    remainder, coupling, turned = remove(wall, xrel, slab, coupling, turned)
    return (turned.T, coupling, remainder)


def solution(mesh):
    placed = (P("prow", "pcol"), P("prow", "pcol"))
    return jax.shard_map(
        functools.partial(per_device, mesh.shape["prow"], mesh.shape["pcol"]),
        mesh=mesh,
        in_specs=placed,
        out_specs=(P(None, "pcol"), P(None, "pcol"), P("prow", "pcol")),
        check_vma=False,
    )
```

```python
import functools

import jax
import jax.numpy as jnp
from jax import lax
from jax.experimental import pallas as pl
from jax.experimental.pallas import tpu as pltpu
from jax.sharding import PartitionSpec as P

MESH = pl.DeviceIdType.MESH
N = 512
BLK = 128
GRP = 8
SUB = 32
HI = lax.Precision.HIGHEST
OWN = 2
TILE = (8, 128)
GT = 20
PIECES = 2
UNROLL = True
G0 = 12
PAIRS = ((1, 3), (0, 4), (7, 5), (2, 6))


def split(x):
    high = x.astype(jnp.bfloat16)
    return high, (x - high.astype(jnp.float32)).astype(jnp.bfloat16)


def bdot(left, right, dims):
    return lax.dot_general(left, right, (dims, ((), ())), preferred_element_type=jnp.float32)


def dot3(left, right, dims):
    lhi, llo = split(left)
    rhi, rlo = split(right)
    return bdot(lhi, rhi, dims) + (bdot(lhi, rlo, dims) + bdot(llo, rhi, dims))


def hdot(left, right, dims):
    return lax.dot_general(left, right, (dims, ((), ())), precision=HI, preferred_element_type=jnp.float32)


def factor_block(tile):
    groups = BLK // GRP
    near = SUB // GRP
    lanes = lax.broadcasted_iota(jnp.int32, (GRP, BLK), 1)
    subs = lax.broadcasted_iota(jnp.int32, (GRP, BLK), 0)
    rows = [tile[g * GRP:(g + 1) * GRP, :] for g in range(groups)]
    upper, inverse, scaled_rows, masked_rows = [], [], [], []
    for g in range(groups):
        first = g * GRP
        last = (g // near + 1) * near
        spread = {
            i: [jnp.broadcast_to(rows[i][:, first + k:first + k + 1], (GRP, BLK)) for k in range(GRP)]
            for i in range(g, last)
        }
        pivot = [
            [jnp.broadcast_to(spread[g][k][r:r + 1, :], (GRP, BLK)) if k >= r else None for k in range(GRP)]
            for r in range(GRP)
        ]
        inside = (lanes >= first) & (lanes < first + GRP)
        line = [
            jnp.where(inside, jnp.where(lanes == first + r, 1.0, 0.0), jnp.broadcast_to(rows[g][r:r + 1, :], (GRP, BLK)))
            for r in range(GRP)
        ]
        recips, factors = [], []
        for j in range(GRP):
            recip = 1.0 / pivot[j][j]
            recips.append(recip)
            scaled = [pivot[j][r] * recip if r > j else None for r in range(GRP)]
            factors.append(scaled)
            for r in range(j + 1, GRP):
                for k in range(r, GRP):
                    pivot[r][k] = pivot[r][k] - scaled[r] * pivot[j][k]
                line[r] = line[r] - scaled[r] * line[j]
        if g + 1 < last:
            back = [line[r] * recips[r] for r in range(GRP)]
            for j in range(GRP - 1, -1, -1):
                for r in range(j):
                    back[r] = back[r] - factors[r][j] * back[j]
            for i in range(g + 1, last):
                total = jnp.where(inside, 0.0, rows[i])
                for k in range(GRP):
                    total = total - spread[i][k] * back[k]
                rows[i] = total
        joined = jnp.zeros((GRP, BLK), jnp.float32)
        upright = jnp.zeros((GRP, BLK), jnp.float32)
        for r in range(GRP):
            root = lax.rsqrt(pivot[r][r])
            right = line[r]
            for k in range(r, GRP):
                right = jnp.where(lanes == first + k, pivot[r][k], right)
            joined = jnp.where(subs == r, line[r] * root, joined)
            upright = jnp.where(subs == r, right * root, upright)
        scaled_rows.append(joined)
        masked_rows.append(jnp.where((lanes >= first + GRP) & (lanes < last * GRP), 0.0, joined))
        upper.append(jnp.where(lanes >= first + subs, upright, 0.0))
        inverse.append(jnp.where(lanes <= first + subs, joined, 0.0))
        if g + 1 == last and last < groups:
            begin = (last - near) * GRP
            done = jnp.concatenate(scaled_rows[last - near:last], 0)
            kept = jnp.concatenate(masked_rows[last - near:last], 0)
            change = hdot(done, kept, ((0,), (0,)))
            cleared = (lanes >= begin) & (lanes < last * GRP)
            for i in range(last, groups):
                rows[i] = jnp.where(cleared, 0.0, rows[i]) - change[i * GRP:(i + 1) * GRP, :]
    return jnp.concatenate(upper, 0), jnp.concatenate(inverse, 0)


def carry_rhs(b, inv, upper_ref, work, coupling_ref):
    low, high = b * BLK, (b + 1) * BLK
    part = hdot(inv[b], work[low:high, N:], ((1,), (0,)))
    coupling_ref[low:high, :] = part
    if high < N:
        work[high:, N:] -= dot3(upper_ref[low:high, high:], part, ((0,), (0,)))


def factor_all(work, inv, upper_ref, after):
    blocks = N // BLK

    def body(k, carry):
        start = k * BLK
        upper, inverse = factor_block(work[pl.ds(start, BLK), pl.ds(start, BLK)])
        inv[k] = inverse
        upper_ref[pl.ds(start, BLK), pl.ds(start, BLK)] = upper
        for b in range(blocks):
            if k == b:
                low, high = b * BLK, (b + 1) * BLK
                dims = ((0,), (0,))
                if high < N:
                    across = hdot(inv[b], work[low:high, high:N], ((1,), (0,)))
                    upper_ref[low:high, high:] = across
                    for c in range(b + 1, blocks):
                        top = c * BLK - high
                        work[c * BLK:(c + 1) * BLK, c * BLK:N] -= dot3(across[:, top:top + BLK], across[:, top:], dims)
                after(b)
        return carry

    for k in range(blocks):
        body(k, 0)


def back_solve(inv, upper_ref, coupling_ref, x_ref):
    blocks = N // BLK
    for k in range(blocks - 1, -1, -1):
        rhs = coupling_ref[k * BLK:(k + 1) * BLK, :]
        if k < blocks - 1:
            rhs = rhs - dot3(upper_ref[k * BLK:(k + 1) * BLK, (k + 1) * BLK:], x_ref[(k + 1) * BLK:, :], ((1,), (0,)))
        x_ref[k * BLK:(k + 1) * BLK, :] = dot3(inv[k], rhs, ((0,), (0,)))


def assemble(gall, work):
    def part(i, d):
        p = (i + (1 if d < 3 else 2)) % 8
        first = (0, 0, 8, G0, G0)[d]
        count = 4 if d == 2 else 8
        both = jnp.concatenate([gall[first + t, p] for t in range(count)], 0)
        if d == 2:
            return jnp.concatenate([both[:, :64], both[:, 64:]], 0)
        side = 64 * (0, 1, 0, 0, 1)[d]
        return both[:, side:side + 64]

    def block(a, b):
        if a > b:
            return block(b, a).T
        if b - a <= 4:
            return part(a, b - a)
        return part(b, 8 - (b - a)).T

    for a in range(8):
        for pair in range(a // 2, 4):
            work[64 * a:64 * a + 64, 128 * pair:128 * pair + 128] = jnp.concatenate(
                [block(a, 2 * pair), block(a, 2 * pair + 1)], 1
            )


def gram_owner(q):
    if q < G0:
        return 8 * (q // 3) + (0, 4, 6)[q % 3]
    return 8 * ((q - G0) // 2) + (1, 3)[(q - G0) % 2]


def main_kernel(
    wt_ref, slab_ref, wall, xrel_ref, coupling_ref, rt_ref,
    gall, sfull, slab, shi, slo, spart, srecv, gpart, grecv, gz, span, work, upper_ref, inv, x_ref, turned,
    load_sem, plus_send, plus_recv, minus_send, minus_recv,
    s_send, s_recv, a_send, a_recv, g_send, g_recv, z_send, z_recv, h_send, h_recv, p_send, p_recv,
    *, rows, planes,
):
    r = lax.axis_index("prow")
    z = lax.axis_index("pcol")
    wide = wt_ref.shape[1]
    half = wide // PIECES
    right, left = lax.rem(z + 1, planes), lax.rem(z + planes - 1, planes)
    core, spot, line = lax.rem(r, 2), lax.rem(r, 8), lax.div(r, 8)
    reducer = ((core == 0) & (spot != 2)) | ((core == 1) & (spot < 4))
    near = lax.div(spot, 2)
    place = jnp.where(core == 0, 3 * line + near - jnp.minimum(near, 1), G0 + 2 * line + near)

    load = pltpu.make_async_copy(slab_ref, slab, load_sem.at[0])
    load.start()
    own = pltpu.make_async_copy(wt_ref, wall.at[OWN], load_sem.at[1])
    own.start()

    barrier = pltpu.get_barrier_semaphore()

    def greet_row(o, c):
        pl.semaphore_signal(barrier, inc=1, device_id=(lax.rem(r + o, rows), z), device_id_type=MESH)
        return c

    def greet_plane(o, c):
        pl.semaphore_signal(barrier, inc=1, device_id=(r, lax.rem(z + o, planes)), device_id_type=MESH)
        return c

    lax.fori_loop(1, planes, greet_plane, 0, unroll=UNROLL)
    lax.fori_loop(1, rows, greet_row, 0, unroll=UNROLL)
    pl.semaphore_wait(barrier, rows - 1 + planes - 1)

    def piece(h):
        return pl.ds(h * half, half)

    plus_slot = [OWN, 1, 0, 7, 6]
    minus_slot = [OWN, 3, 4, 5, 6]

    def hop(step, h, plus):
        slots = plus_slot if plus else minus_slot
        src = wt_ref if step == 1 else wall.at[slots[step - 1]]
        send, recv = (plus_send, plus_recv) if plus else (minus_send, minus_recv)
        n = PIECES * (step - 1) + h
        return pltpu.make_async_remote_copy(
            src_ref=src.at[:, piece(h)],
            dst_ref=wall.at[slots[step], :, piece(h)],
            send_sem=send.at[n],
            recv_sem=recv.at[n],
            device_id=(r, right if plus else left),
            device_id_type=MESH,
        )

    hops = {}
    for step in (1, 2, 3):
        for h in range(PIECES):
            for plus in (True, False):
                hops[step, h, plus] = hop(step, h, plus)
    for h in range(PIECES // 2):
        hops[4, h, True] = hop(4, h, True)
        hops[4, h + PIECES // 2, False] = hop(4, h + PIECES // 2, False)

    def forward(step, parts=tuple(range(PIECES))):
        for h in parts:
            for plus in (True, False):
                hops[step, h, plus].wait_recv()
                if (step + 1, h, plus) in hops:
                    hops[step + 1, h, plus].start()

    for h in range(PIECES):
        for plus in (True, False):
            hops[1, h, plus].start()

    def tiles_out(acc, g, base):
        for t in range(acc.shape[0] // 8 * 2):
            spart[g, base + t] = acc[8 * (t // 2):8 * (t // 2) + 8, 128 * (t % 2):128 * (t % 2) + 128]

    def product(slots):
        parts = [split(wall[k]) for k in slots]
        highs = [p[0] for p in parts]
        n = 64 * len(slots)
        both = bdot(jnp.concatenate(highs + [p[1] for p in parts], 0), shi[...], ((1,), (0,)))
        cross = bdot(jnp.concatenate(highs, 0), slo[...], ((1,), (0,)))
        return both[:n] + both[n:] + cross

    def scatter(part, recv_buf, send, recv):
        recv_at = recv_buf.at[r]

        def body(o, c):
            t = lax.rem(r + o, rows)
            pltpu.make_async_remote_copy(
                src_ref=part.at[t], dst_ref=recv_at, send_sem=send, recv_sem=recv,
                device_id=(t, z), device_id_type=MESH,
            ).start()
            return c

        lax.fori_loop(1, rows, body, 0, unroll=UNROLL)

    def drain(ref, sem):
        pltpu.make_async_copy(ref, ref, sem).wait()

    def s_scatter(g):
        srecv[g, r] = spart[g, r]
        scatter(spart.at[g], srecv.at[g], s_send.at[g], s_recv.at[g])

    def s_gather(g):
        drain(srecv.at[g, pl.ds(0, rows - 1)], s_recv.at[g])
        total = srecv[g, 0]
        for q in range(1, rows):
            total = total + srecv[g, q]
        sfull[g, r] = total

        def body(o, c):
            pltpu.make_async_remote_copy(
                src_ref=sfull.at[g, r], dst_ref=sfull.at[g, r], send_sem=a_send.at[g], recv_sem=a_recv.at[g],
                device_id=(lax.rem(r + o, rows), z), device_id_type=MESH,
            ).start()
            return c

        lax.fori_loop(1, rows, body, 0, unroll=UNROLL)

    def gram_scatter(c):
        first_slot, others = ((1, (1, 2, 3)), (0, (3, 4)))[c]
        vhi, vlo = split(wall[first_slot])
        seen = [split(wall[k]) for k in others]
        first = bdot(jnp.concatenate([vhi, vlo], 0), jnp.concatenate([w[0] for w in seen], 0), ((1,), (1,)))
        second = bdot(vhi, jnp.concatenate([w[1] for w in seen], 0), ((1,), (1,)))
        acc = first[:64] + first[64:] + second
        packed = [acc[:, :128]]
        if c == 0:
            packed.append(jnp.concatenate([acc[:32, 128:], acc[32:, 128:]], 1))
        n = c * G0
        for p in packed:
            for t in range(p.shape[0] // 8):
                gpart[n] = p[8 * t:8 * t + 8]
                n += 1

        @pl.when(reducer & (core == c))
        def _():
            grecv[r] = gpart[place]

        for q in range(*((0, G0), (G0, GT))[c]):
            @pl.when(r != gram_owner(q))
            def _():
                pltpu.make_async_remote_copy(
                    src_ref=gpart.at[q], dst_ref=grecv.at[r], send_sem=g_send.at[0], recv_sem=g_recv.at[0],
                    device_id=(gram_owner(q), z), device_id_type=MESH,
                ).start()

    def gram_across(c):
        @pl.when(reducer & (core == c))
        def _():
            drain(grecv.at[pl.ds(0, rows - 1)], g_recv.at[0])
            total = grecv[0]
            for q in range(1, rows):
                total = total + grecv[q]
            gz[z] = total

            def body(o, carry):
                pltpu.make_async_remote_copy(
                    src_ref=gz.at[z], dst_ref=gz.at[z], send_sem=z_send.at[0], recv_sem=z_recv.at[0],
                    device_id=(r, lax.rem(z + o, planes)), device_id_type=MESH,
                ).start()
                return carry

            lax.fori_loop(1, planes, body, 0, unroll=UNROLL)

    def gram_gather(c):
        @pl.when(reducer & (core == c))
        def _():
            drain(gz.at[pl.ds(0, planes - 1)], z_recv.at[0])
            gall[place] = gz[...]

            def body(o, carry):
                pltpu.make_async_remote_copy(
                    src_ref=gz, dst_ref=gall.at[place], send_sem=h_send.at[0], recv_sem=h_recv.at[0],
                    device_id=(lax.rem(r + 2 * o, rows), z), device_id_type=MESH,
                ).start()
                return carry

            lax.fori_loop(1, rows // 2, body, 0, unroll=UNROLL)

    parts_of = (gall.at[pl.ds(0, G0)], gall.at[pl.ds(G0, GT - G0)])

    def pair_copy(c):
        return pltpu.make_async_remote_copy(
            src_ref=parts_of[c], dst_ref=parts_of[c], send_sem=p_send.at[0], recv_sem=p_recv.at[0],
            device_id=(r + 1 - 2 * c, z), device_id_type=MESH,
        )

    def gram_pair(c):
        count = (G0, GT - G0)[c]

        @pl.when((core == c) & reducer)
        def _():
            drain(gall.at[pl.ds(0, count - 1)], h_recv.at[0])

        @pl.when((core == c) & jnp.logical_not(reducer))
        def _():
            drain(gall.at[pl.ds(0, count)], h_recv.at[0])

        @pl.when(core == c)
        def _():
            pair_copy(c).start()

    def gram_wait():
        for c in (0, 1):
            @pl.when(core == c)
            def _():
                drain(parts_of[1 - c], p_recv.at[0])

    def s_place():
        for g in range(4):
            drain(sfull.at[g, pl.ds(0, rows - 1)], a_recv.at[g])
        for g in range(4):
            for t in range(32):
                base = 64 * lax.rem(z + 6 + PAIRS[g][t // 16], 8) + 8 * ((t // 2) % 8)
                work[pl.ds(pl.multiple_of(base, 8), 8), N + 128 * (t % 2):N + 128 * (t % 2) + 128] = sfull[g, t]

    def after(b):
        if b == 0:
            for h in range(PIECES // 2):
                hops[4, h, True].wait_recv()
                hops[4, h + PIECES // 2, False].wait_recv()
            tiles_out(product((6,)), 3, 16)
            s_scatter(3)
            s_gather(1)
            s_gather(2)
        if b == 1:
            s_gather(3)
        if b == 2:
            s_place()
            for c in range(3):
                carry_rhs(c, inv, upper_ref, work, coupling_ref)
        if b == 3:
            carry_rhs(3, inv, upper_ref, work, coupling_ref)

    load.wait()
    own.wait()
    high, low = split(slab[...])
    shi[...] = high
    slo[...] = low
    tiles_out(product((OWN,)), 3, 0)

    forward(1)
    gram_scatter(0)
    tiles_out(product(PAIRS[0]), 0, 0)
    gram_across(0)
    s_scatter(0)
    forward(2, (0,))
    gram_gather(0)
    forward(2, (1,))
    gram_scatter(1)
    tiles_out(product(PAIRS[1]), 1, 0)
    gram_across(1)
    s_scatter(1)
    s_gather(0)
    gram_pair(0)
    forward(3, (0,))
    gram_gather(1)
    forward(3, (1,))
    tiles_out(product(PAIRS[2]), 2, 0)
    s_scatter(2)
    gram_pair(1)
    upper_ref[...] = jnp.zeros_like(upper_ref)
    gram_wait()
    assemble(gall, work)
    factor_all(work, inv, upper_ref, after)
    back_solve(inv, upper_ref, coupling_ref, x_ref)
    for b in range(8):
        slot = lax.rem(b + 10 - z, 8)
        xrel_ref[pl.ds(pl.multiple_of(64 * slot, 64), 64), :] = x_ref[64 * b:64 * b + 64, :]
    first = pl.multiple_of(lax.div(z, 2) * 128, 128)
    turned[...] = upper_ref[:, pl.ds(first, 128)].T
    rt_ref[...] = turned[pl.ds(pl.multiple_of(64 * lax.rem(z, 2), 64), 64), :]

    for copy in hops.values():
        copy.wait_send()
    for g in range(4):
        drain(spart.at[g, pl.ds(0, rows - 1)], s_send.at[g])
        drain(sfull.at[g, pl.ds(0, rows - 1)], a_send.at[g])

    @pl.when(reducer)
    def _():
        drain(gpart.at[pl.ds(0, GT - 1)], g_send.at[0])
        drain(gz.at[pl.ds(0, planes - 1)], z_send.at[0])
        drain(span, h_send.at[0])

    @pl.when(jnp.logical_not(reducer))
    def _():
        drain(gpart, g_send.at[0])

    for c in (0, 1):
        @pl.when(core == c)
        def _():
            drain(parts_of[c], p_send.at[0])


def window(wt, slab, rows, planes):
    depth, width = slab.shape
    hbm = pl.BlockSpec(memory_space=pltpu.HBM)
    vmem = pl.BlockSpec(memory_space=pltpu.VMEM)
    f32 = jnp.float32
    dma = pltpu.SemaphoreType.DMA
    return pl.pallas_call(
        functools.partial(main_kernel, rows=rows, planes=planes),
        out_shape=(
            jax.ShapeDtypeStruct((planes, wt.shape[0], depth), f32),
            jax.ShapeDtypeStruct((N, width), f32),
            jax.ShapeDtypeStruct((N, width), f32),
            jax.ShapeDtypeStruct((64, N), f32),
        ),
        in_specs=[hbm] * 2,
        out_specs=(vmem,) * 4,
        scratch_shapes=[
            pltpu.VMEM((GT, planes) + TILE, f32),
            pltpu.VMEM((4, rows) + TILE, f32),
            pltpu.VMEM((depth, width), f32),
            pltpu.VMEM((depth, width), jnp.bfloat16),
            pltpu.VMEM((depth, width), jnp.bfloat16),
            pltpu.VMEM((4, rows) + TILE, f32),
            pltpu.VMEM((4, rows) + TILE, f32),
            pltpu.VMEM((GT,) + TILE, f32),
            pltpu.VMEM((rows,) + TILE, f32),
            pltpu.VMEM((planes,) + TILE, f32),
            pltpu.VMEM((rows // 2 - 1, planes) + TILE, f32),
            pltpu.VMEM((N, N + width), f32),
            pltpu.VMEM((N, N), f32),
            pltpu.VMEM((N // BLK, BLK, BLK), f32),
            pltpu.VMEM((N, width), f32),
            pltpu.VMEM((BLK, N), f32),
            dma((2,)), dma((4 * PIECES,)), dma((4 * PIECES,)), dma((4 * PIECES,)), dma((4 * PIECES,)),
            dma((4,)), dma((4,)), dma((4,)), dma((4,)),
            dma((1,)), dma((1,)), dma((1,)), dma((1,)), dma((1,)), dma((1,)), dma((1,)), dma((1,)),
        ],
        compiler_params=pltpu.CompilerParams(
            collective_id=0, has_side_effects=True, vmem_limit_bytes=40 << 20
        ),
    )(wt, slab)


def remainder_kernel(wall, x_ref, slab_ref, coupling_in, rt_in, out_ref, coupling_out, rt_out, xhi, xlo):
    coupling_out[...] = coupling_in[...]
    rt_out[...] = rt_in[...]

    @pl.when(pl.program_id(0) == 0)
    def _():
        high, low = split(x_ref[...])
        xhi[...] = high
        xlo[...] = low

    whi, wlo = split(wall[...].reshape(N, wall.shape[2]))
    dims = ((0,), (0,))
    moved = bdot(whi, xhi[...], dims) + bdot(wlo, xhi[...], dims) + bdot(whi, xlo[...], dims)
    out_ref[...] = slab_ref[...] - moved


def remove(wall, xrel, slab, coupling, turned):
    rows, width = slab.shape
    tile = 512
    steps = rows // tile
    f32 = jnp.float32
    slab_spec = pl.BlockSpec((tile, width), lambda i: (i, 0))
    coupling_spec = pl.BlockSpec((N // steps, width), lambda i: (i, 0))
    turned_spec = pl.BlockSpec((turned.shape[0] // steps, N), lambda i: (i, 0))
    return pl.pallas_call(
        remainder_kernel,
        out_shape=(
            jax.ShapeDtypeStruct((rows, width), f32),
            jax.ShapeDtypeStruct(coupling.shape, f32),
            jax.ShapeDtypeStruct(turned.shape, f32),
        ),
        grid=(steps,),
        in_specs=[
            pl.BlockSpec((wall.shape[0], wall.shape[1], tile), lambda i: (0, 0, i)),
            pl.BlockSpec((N, width), lambda i: (0, 0)),
            slab_spec, coupling_spec, turned_spec,
        ],
        out_specs=(slab_spec, coupling_spec, turned_spec),
        scratch_shapes=[pltpu.VMEM((N, width), jnp.bfloat16), pltpu.VMEM((N, width), jnp.bfloat16)],
        compiler_params=pltpu.CompilerParams(vmem_limit_bytes=24 << 20),
    )(wall, xrel, slab, coupling, turned)


def per_device(rows, planes, panels, slab):
    wall, xrel, coupling, turned = window(pltpu.with_memory_space_constraint(panels.T, pltpu.HBM), pltpu.with_memory_space_constraint(slab, pltpu.HBM), rows, planes)
    remainder, coupling, turned = remove(wall, xrel, slab, coupling, turned)
    return (turned.T, coupling, remainder)


def solution(mesh):
    placed = (P("prow", "pcol"), P("prow", "pcol"))
    return jax.shard_map(
        functools.partial(per_device, mesh.shape["prow"], mesh.shape["pcol"]),
        mesh=mesh,
        in_specs=placed,
        out_specs=(P(None, "pcol"), P(None, "pcol"), P("prow", "pcol")),
        check_vma=False,
    )
```

```python
import functools

import jax
import jax.numpy as jnp
from jax import lax
from jax.experimental import pallas as pl
from jax.experimental.pallas import tpu as pltpu
from jax.sharding import PartitionSpec as P

MESH = pl.DeviceIdType.MESH
N = 512
BLK = 128
GRP = 8
SUB = 32
HI = lax.Precision.HIGHEST
OWN = 2
TILE = (8, 128)
GT = 20
PIECES = 2
UNROLL = True
G0 = 12
PAIRS = ((1, 3), (0, 4), (7, 5), (2, 6))


def split(x):
    high = x.astype(jnp.bfloat16)
    return high, (x - high.astype(jnp.float32)).astype(jnp.bfloat16)


def bdot(left, right, dims):
    return lax.dot_general(left, right, (dims, ((), ())), preferred_element_type=jnp.float32)


def dot3(left, right, dims):
    lhi, llo = split(left)
    rhi, rlo = split(right)
    return bdot(lhi, rhi, dims) + (bdot(lhi, rlo, dims) + bdot(llo, rhi, dims))


def hdot(left, right, dims):
    return lax.dot_general(left, right, (dims, ((), ())), precision=HI, preferred_element_type=jnp.float32)


def factor_block(tile):
    groups = BLK // GRP
    near = SUB // GRP
    lanes = lax.broadcasted_iota(jnp.int32, (GRP, BLK), 1)
    subs = lax.broadcasted_iota(jnp.int32, (GRP, BLK), 0)
    rows = [tile[g * GRP:(g + 1) * GRP, :] for g in range(groups)]
    upper, inverse, scaled_rows, masked_rows = [], [], [], []
    for g in range(groups):
        first = g * GRP
        last = (g // near + 1) * near
        spread = {
            i: [jnp.broadcast_to(rows[i][:, first + k:first + k + 1], (GRP, BLK)) for k in range(GRP)]
            for i in range(g, last)
        }
        pivot = [
            [jnp.broadcast_to(spread[g][k][r:r + 1, :], (GRP, BLK)) if k >= r else None for k in range(GRP)]
            for r in range(GRP)
        ]
        inside = (lanes >= first) & (lanes < first + GRP)
        line = [
            jnp.where(inside, jnp.where(lanes == first + r, 1.0, 0.0), jnp.broadcast_to(rows[g][r:r + 1, :], (GRP, BLK)))
            for r in range(GRP)
        ]
        recips, factors = [], []
        for j in range(GRP):
            recip = 1.0 / pivot[j][j]
            recips.append(recip)
            scaled = [pivot[j][r] * recip if r > j else None for r in range(GRP)]
            factors.append(scaled)
            for r in range(j + 1, GRP):
                for k in range(r, GRP):
                    pivot[r][k] = pivot[r][k] - scaled[r] * pivot[j][k]
                line[r] = line[r] - scaled[r] * line[j]
        if g + 1 < last:
            back = [line[r] * recips[r] for r in range(GRP)]
            for j in range(GRP - 1, -1, -1):
                for r in range(j):
                    back[r] = back[r] - factors[r][j] * back[j]
            for i in range(g + 1, last):
                total = jnp.where(inside, 0.0, rows[i])
                for k in range(GRP):
                    total = total - spread[i][k] * back[k]
                rows[i] = total
        joined = jnp.zeros((GRP, BLK), jnp.float32)
        upright = jnp.zeros((GRP, BLK), jnp.float32)
        for r in range(GRP):
            root = lax.rsqrt(pivot[r][r])
            right = line[r]
            for k in range(r, GRP):
                right = jnp.where(lanes == first + k, pivot[r][k], right)
            joined = jnp.where(subs == r, line[r] * root, joined)
            upright = jnp.where(subs == r, right * root, upright)
        scaled_rows.append(joined)
        masked_rows.append(jnp.where((lanes >= first + GRP) & (lanes < last * GRP), 0.0, joined))
        upper.append(jnp.where(lanes >= first + subs, upright, 0.0))
        inverse.append(jnp.where(lanes <= first + subs, joined, 0.0))
        if g + 1 == last and last < groups:
            begin = (last - near) * GRP
            done = jnp.concatenate(scaled_rows[last - near:last], 0)
            kept = jnp.concatenate(masked_rows[last - near:last], 0)
            change = dot3(done, kept, ((0,), (0,)))
            cleared = (lanes >= begin) & (lanes < last * GRP)
            for i in range(last, groups):
                rows[i] = jnp.where(cleared, 0.0, rows[i]) - change[i * GRP:(i + 1) * GRP, :]
    return jnp.concatenate(upper, 0), jnp.concatenate(inverse, 0)


def carry_rhs(b, inv, upper_ref, work, coupling_ref):
    low, high = b * BLK, (b + 1) * BLK
    part = hdot(inv[b], work[low:high, N:], ((1,), (0,)))
    coupling_ref[low:high, :] = part
    if high < N:
        work[high:, N:] -= dot3(upper_ref[low:high, high:], part, ((0,), (0,)))


def factor_all(work, inv, upper_ref, after):
    blocks = N // BLK

    def body(k, carry):
        start = k * BLK
        upper, inverse = factor_block(work[pl.ds(start, BLK), pl.ds(start, BLK)])
        inv[k] = inverse
        upper_ref[pl.ds(start, BLK), pl.ds(start, BLK)] = upper
        for b in range(blocks):
            if k == b:
                low, high = b * BLK, (b + 1) * BLK
                dims = ((0,), (0,))
                if high < N:
                    across = hdot(inv[b], work[low:high, high:N], ((1,), (0,)))
                    upper_ref[low:high, high:] = across
                    for c in range(b + 1, blocks):
                        top = c * BLK - high
                        work[c * BLK:(c + 1) * BLK, c * BLK:N] -= dot3(across[:, top:top + BLK], across[:, top:], dims)
                after(b)
        return carry

    for k in range(blocks):
        body(k, 0)


def back_solve(inv, upper_ref, coupling_ref, x_ref):
    blocks = N // BLK
    for k in range(blocks - 1, -1, -1):
        rhs = coupling_ref[k * BLK:(k + 1) * BLK, :]
        if k < blocks - 1:
            rhs = rhs - dot3(upper_ref[k * BLK:(k + 1) * BLK, (k + 1) * BLK:], x_ref[(k + 1) * BLK:, :], ((1,), (0,)))
        x_ref[k * BLK:(k + 1) * BLK, :] = dot3(inv[k], rhs, ((0,), (0,)))


def assemble(gall, work):
    def part(i, d):
        p = (i + (1 if d < 3 else 2)) % 8
        first = (0, 0, 8, G0, G0)[d]
        count = 4 if d == 2 else 8
        both = jnp.concatenate([gall[first + t, p] for t in range(count)], 0)
        if d == 2:
            return jnp.concatenate([both[:, :64], both[:, 64:]], 0)
        side = 64 * (0, 1, 0, 0, 1)[d]
        return both[:, side:side + 64]

    def block(a, b):
        if a > b:
            return block(b, a).T
        if b - a <= 4:
            return part(a, b - a)
        return part(b, 8 - (b - a)).T

    for a in range(8):
        for pair in range(a // 2, 4):
            work[64 * a:64 * a + 64, 128 * pair:128 * pair + 128] = jnp.concatenate(
                [block(a, 2 * pair), block(a, 2 * pair + 1)], 1
            )


def gram_owner(q):
    if q < G0:
        return 8 * (q // 3) + (0, 4, 6)[q % 3]
    return 8 * ((q - G0) // 2) + (1, 3)[(q - G0) % 2]


def main_kernel(
    wt_ref, slab_ref, whi, wlo, xrel_ref, coupling_ref, rt_ref,
    wall, gall, sfull, slab, shi, slo, spart, srecv, gpart, grecv, gz, span, work, upper_ref, inv, x_ref, turned,
    load_sem, plus_send, plus_recv, minus_send, minus_recv,
    s_send, s_recv, a_send, a_recv, g_send, g_recv, z_send, z_recv, h_send, h_recv, p_send, p_recv,
    *, rows, planes,
):
    r = lax.axis_index("prow")
    z = lax.axis_index("pcol")
    wide = wt_ref.shape[1]
    half = wide // PIECES
    right, left = lax.rem(z + 1, planes), lax.rem(z + planes - 1, planes)
    core, spot, line = lax.rem(r, 2), lax.rem(r, 8), lax.div(r, 8)
    reducer = ((core == 0) & (spot != 2)) | ((core == 1) & (spot < 4))
    near = lax.div(spot, 2)
    place = jnp.where(core == 0, 3 * line + near - jnp.minimum(near, 1), G0 + 2 * line + near)

    load = pltpu.make_async_copy(slab_ref, slab, load_sem.at[0])
    load.start()
    own = pltpu.make_async_copy(wt_ref, wall.at[OWN], load_sem.at[1])
    own.start()

    barrier = pltpu.get_barrier_semaphore()

    def greet_row(o, c):
        pl.semaphore_signal(barrier, inc=1, device_id=(lax.rem(r + o, rows), z), device_id_type=MESH)
        return c

    def greet_plane(o, c):
        pl.semaphore_signal(barrier, inc=1, device_id=(r, lax.rem(z + o, planes)), device_id_type=MESH)
        return c

    lax.fori_loop(1, planes, greet_plane, 0, unroll=UNROLL)
    lax.fori_loop(1, rows, greet_row, 0, unroll=UNROLL)
    pl.semaphore_wait(barrier, rows - 1 + planes - 1)

    def piece(h):
        return pl.ds(h * half, half)

    plus_slot = [OWN, 1, 0, 7, 6]
    minus_slot = [OWN, 3, 4, 5, 6]

    def hop(step, h, plus):
        slots = plus_slot if plus else minus_slot
        src = wt_ref if step == 1 else wall.at[slots[step - 1]]
        send, recv = (plus_send, plus_recv) if plus else (minus_send, minus_recv)
        n = PIECES * (step - 1) + h
        return pltpu.make_async_remote_copy(
            src_ref=src.at[:, piece(h)],
            dst_ref=wall.at[slots[step], :, piece(h)],
            send_sem=send.at[n],
            recv_sem=recv.at[n],
            device_id=(r, right if plus else left),
            device_id_type=MESH,
        )

    hops = {}
    for step in (1, 2, 3):
        for h in range(PIECES):
            for plus in (True, False):
                hops[step, h, plus] = hop(step, h, plus)
    for h in range(PIECES // 2):
        hops[4, h, True] = hop(4, h, True)
        hops[4, h + PIECES // 2, False] = hop(4, h + PIECES // 2, False)

    def forward(step, parts=tuple(range(PIECES))):
        for h in parts:
            for plus in (True, False):
                hops[step, h, plus].wait_recv()
                if (step + 1, h, plus) in hops:
                    hops[step + 1, h, plus].start()

    for h in range(PIECES):
        for plus in (True, False):
            hops[1, h, plus].start()

    def tiles_out(acc, g, base):
        for t in range(acc.shape[0] // 8 * 2):
            spart[g, base + t] = acc[8 * (t // 2):8 * (t // 2) + 8, 128 * (t % 2):128 * (t % 2) + 128]

    def keep(*slots):
        for k in slots:
            whi[k], wlo[k] = split(wall[k])

    def product(slots):
        highs = [whi[k] for k in slots]
        n = 64 * len(slots)
        both = bdot(jnp.concatenate(highs + [wlo[k] for k in slots], 0), shi[...], ((1,), (0,)))
        cross = bdot(jnp.concatenate(highs, 0), slo[...], ((1,), (0,)))
        return both[:n] + both[n:] + cross

    def scatter(part, recv_buf, send, recv):
        recv_at = recv_buf.at[r]

        def body(o, c):
            t = lax.rem(r + o, rows)
            pltpu.make_async_remote_copy(
                src_ref=part.at[t], dst_ref=recv_at, send_sem=send, recv_sem=recv,
                device_id=(t, z), device_id_type=MESH,
            ).start()
            return c

        lax.fori_loop(1, rows, body, 0, unroll=UNROLL)

    def drain(ref, sem):
        pltpu.make_async_copy(ref, ref, sem).wait()

    def s_scatter(g):
        srecv[g, r] = spart[g, r]
        scatter(spart.at[g], srecv.at[g], s_send.at[g], s_recv.at[g])

    def s_gather(g):
        drain(srecv.at[g, pl.ds(0, rows - 1)], s_recv.at[g])
        total = srecv[g, 0]
        for q in range(1, rows):
            total = total + srecv[g, q]
        sfull[g, r] = total

        def body(o, c):
            pltpu.make_async_remote_copy(
                src_ref=sfull.at[g, r], dst_ref=sfull.at[g, r], send_sem=a_send.at[g], recv_sem=a_recv.at[g],
                device_id=(lax.rem(r + o, rows), z), device_id_type=MESH,
            ).start()
            return c

        lax.fori_loop(1, rows, body, 0, unroll=UNROLL)

    def gram_scatter(c):
        first_slot, others = ((1, (1, 2, 3)), (0, (3, 4)))[c]
        vhi, vlo = whi[first_slot], wlo[first_slot]
        seen = [(whi[k], wlo[k]) for k in others]
        first = bdot(jnp.concatenate([vhi, vlo], 0), jnp.concatenate([w[0] for w in seen], 0), ((1,), (1,)))
        second = bdot(vhi, jnp.concatenate([w[1] for w in seen], 0), ((1,), (1,)))
        acc = first[:64] + first[64:] + second
        packed = [acc[:, :128]]
        if c == 0:
            packed.append(jnp.concatenate([acc[:32, 128:], acc[32:, 128:]], 1))
        n = c * G0
        for p in packed:
            for t in range(p.shape[0] // 8):
                gpart[n] = p[8 * t:8 * t + 8]
                n += 1

        @pl.when(reducer & (core == c))
        def _():
            grecv[r] = gpart[place]

        for q in range(*((0, G0), (G0, GT))[c]):
            @pl.when(r != gram_owner(q))
            def _():
                pltpu.make_async_remote_copy(
                    src_ref=gpart.at[q], dst_ref=grecv.at[r], send_sem=g_send.at[0], recv_sem=g_recv.at[0],
                    device_id=(gram_owner(q), z), device_id_type=MESH,
                ).start()

    def gram_across(c):
        @pl.when(reducer & (core == c))
        def _():
            drain(grecv.at[pl.ds(0, rows - 1)], g_recv.at[0])
            total = grecv[0]
            for q in range(1, rows):
                total = total + grecv[q]
            gz[z] = total

            def body(o, carry):
                pltpu.make_async_remote_copy(
                    src_ref=gz.at[z], dst_ref=gz.at[z], send_sem=z_send.at[0], recv_sem=z_recv.at[0],
                    device_id=(r, lax.rem(z + o, planes)), device_id_type=MESH,
                ).start()
                return carry

            lax.fori_loop(1, planes, body, 0, unroll=UNROLL)

    def gram_gather(c):
        @pl.when(reducer & (core == c))
        def _():
            drain(gz.at[pl.ds(0, planes - 1)], z_recv.at[0])
            gall[place] = gz[...]

            def body(o, carry):
                pltpu.make_async_remote_copy(
                    src_ref=gz, dst_ref=gall.at[place], send_sem=h_send.at[0], recv_sem=h_recv.at[0],
                    device_id=(lax.rem(r + 2 * o, rows), z), device_id_type=MESH,
                ).start()
                return carry

            lax.fori_loop(1, rows // 2, body, 0, unroll=UNROLL)

    parts_of = (gall.at[pl.ds(0, G0)], gall.at[pl.ds(G0, GT - G0)])

    def pair_copy(c):
        return pltpu.make_async_remote_copy(
            src_ref=parts_of[c], dst_ref=parts_of[c], send_sem=p_send.at[0], recv_sem=p_recv.at[0],
            device_id=(r + 1 - 2 * c, z), device_id_type=MESH,
        )

    def gram_pair(c):
        count = (G0, GT - G0)[c]

        @pl.when((core == c) & reducer)
        def _():
            drain(gall.at[pl.ds(0, count - 1)], h_recv.at[0])

        @pl.when((core == c) & jnp.logical_not(reducer))
        def _():
            drain(gall.at[pl.ds(0, count)], h_recv.at[0])

        @pl.when(core == c)
        def _():
            pair_copy(c).start()

    def gram_wait():
        for c in (0, 1):
            @pl.when(core == c)
            def _():
                drain(parts_of[1 - c], p_recv.at[0])

    def s_place():
        for g in range(4):
            drain(sfull.at[g, pl.ds(0, rows - 1)], a_recv.at[g])
        for g in range(4):
            for t in range(32):
                base = 64 * lax.rem(z + 6 + PAIRS[g][t // 16], 8) + 8 * ((t // 2) % 8)
                work[pl.ds(pl.multiple_of(base, 8), 8), N + 128 * (t % 2):N + 128 * (t % 2) + 128] = sfull[g, t]

    def after(b):
        if b == 0:
            for h in range(PIECES // 2):
                hops[4, h, True].wait_recv()
                hops[4, h + PIECES // 2, False].wait_recv()
            keep(6)
            tiles_out(product((6,)), 3, 16)
            s_scatter(3)
            s_gather(1)
            s_gather(2)
        if b == 1:
            s_gather(3)
        if b == 2:
            s_place()
            for c in range(3):
                carry_rhs(c, inv, upper_ref, work, coupling_ref)
        if b == 3:
            carry_rhs(3, inv, upper_ref, work, coupling_ref)

    load.wait()
    own.wait()
    high, low = split(slab[...])
    shi[...] = high
    slo[...] = low
    keep(OWN)
    tiles_out(product((OWN,)), 3, 0)

    forward(1)
    keep(1, 3)
    gram_scatter(0)
    tiles_out(product(PAIRS[0]), 0, 0)
    gram_across(0)
    s_scatter(0)
    forward(2, (0,))
    gram_gather(0)
    forward(2, (1,))
    keep(0, 4)
    gram_scatter(1)
    tiles_out(product(PAIRS[1]), 1, 0)
    gram_across(1)
    s_scatter(1)
    s_gather(0)
    gram_pair(0)
    forward(3, (0,))
    gram_gather(1)
    forward(3, (1,))
    keep(7, 5)
    tiles_out(product(PAIRS[2]), 2, 0)
    s_scatter(2)
    gram_pair(1)
    upper_ref[...] = jnp.zeros_like(upper_ref)
    gram_wait()
    assemble(gall, work)
    factor_all(work, inv, upper_ref, after)
    back_solve(inv, upper_ref, coupling_ref, x_ref)
    for b in range(8):
        slot = lax.rem(b + 10 - z, 8)
        xrel_ref[pl.ds(pl.multiple_of(64 * slot, 64), 64), :] = x_ref[64 * b:64 * b + 64, :]
    first = pl.multiple_of(lax.div(z, 2) * 128, 128)
    turned[...] = upper_ref[:, pl.ds(first, 128)].T
    rt_ref[...] = turned[pl.ds(pl.multiple_of(64 * lax.rem(z, 2), 64), 64), :]

    for copy in hops.values():
        copy.wait_send()
    for g in range(4):
        drain(spart.at[g, pl.ds(0, rows - 1)], s_send.at[g])
        drain(sfull.at[g, pl.ds(0, rows - 1)], a_send.at[g])

    @pl.when(reducer)
    def _():
        drain(gpart.at[pl.ds(0, GT - 1)], g_send.at[0])
        drain(gz.at[pl.ds(0, planes - 1)], z_send.at[0])
        drain(span, h_send.at[0])

    @pl.when(jnp.logical_not(reducer))
    def _():
        drain(gpart, g_send.at[0])

    for c in (0, 1):
        @pl.when(core == c)
        def _():
            drain(parts_of[c], p_send.at[0])


def window(wt, slab, rows, planes):
    depth, width = slab.shape
    hbm = pl.BlockSpec(memory_space=pltpu.HBM)
    vmem = pl.BlockSpec(memory_space=pltpu.VMEM)
    f32 = jnp.float32
    dma = pltpu.SemaphoreType.DMA
    return pl.pallas_call(
        functools.partial(main_kernel, rows=rows, planes=planes),
        out_shape=(
            jax.ShapeDtypeStruct((planes, wt.shape[0], depth), jnp.bfloat16),
            jax.ShapeDtypeStruct((planes, wt.shape[0], depth), jnp.bfloat16),
            jax.ShapeDtypeStruct((N, width), f32),
            jax.ShapeDtypeStruct((N, width), f32),
            jax.ShapeDtypeStruct((64, N), f32),
        ),
        in_specs=[hbm] * 2,
        out_specs=(vmem,) * 5,
        scratch_shapes=[
            pltpu.VMEM((planes, wt.shape[0], depth), f32),
            pltpu.VMEM((GT, planes) + TILE, f32),
            pltpu.VMEM((4, rows) + TILE, f32),
            pltpu.VMEM((depth, width), f32),
            pltpu.VMEM((depth, width), jnp.bfloat16),
            pltpu.VMEM((depth, width), jnp.bfloat16),
            pltpu.VMEM((4, rows) + TILE, f32),
            pltpu.VMEM((4, rows) + TILE, f32),
            pltpu.VMEM((GT,) + TILE, f32),
            pltpu.VMEM((rows,) + TILE, f32),
            pltpu.VMEM((planes,) + TILE, f32),
            pltpu.VMEM((rows // 2 - 1, planes) + TILE, f32),
            pltpu.VMEM((N, N + width), f32),
            pltpu.VMEM((N, N), f32),
            pltpu.VMEM((N // BLK, BLK, BLK), f32),
            pltpu.VMEM((N, width), f32),
            pltpu.VMEM((BLK, N), f32),
            dma((2,)), dma((4 * PIECES,)), dma((4 * PIECES,)), dma((4 * PIECES,)), dma((4 * PIECES,)),
            dma((4,)), dma((4,)), dma((4,)), dma((4,)),
            dma((1,)), dma((1,)), dma((1,)), dma((1,)), dma((1,)), dma((1,)), dma((1,)), dma((1,)),
        ],
        compiler_params=pltpu.CompilerParams(
            collective_id=0, has_side_effects=True, vmem_limit_bytes=40 << 20
        ),
    )(wt, slab)


def remainder_kernel(
    whi_ref, wlo_ref, x_ref, slab_ref, coupling_in, rt_in, out_ref, coupling_out, rt_out, buffer, sems, *, tile
):
    steps = slab_ref.shape[0] // tile
    small = [
        pltpu.make_async_copy(coupling_in, coupling_out, sems.at[steps]),
        pltpu.make_async_copy(rt_in, rt_out, sems.at[steps + 1]),
    ]
    for copy in small:
        copy.start()
    xhi, xlo = split(x_ref[...])
    dims = ((0,), (0,))
    copies = []
    for i in range(steps):
        piece = pl.ds(i * tile, tile)
        whi = whi_ref[:, :, piece].reshape(N, tile)
        wlo = wlo_ref[:, :, piece].reshape(N, tile)
        moved = bdot(whi, xhi, dims) + bdot(wlo, xhi, dims) + bdot(whi, xlo, dims)
        buffer[piece, :] = slab_ref[piece, :] - moved
        copy = pltpu.make_async_copy(buffer.at[piece, :], out_ref.at[piece, :], sems.at[i])
        copy.start()
        copies.append(copy)
    for copy in small + copies:
        copy.wait()


def remove(whi, wlo, xrel, slab, coupling, turned):
    rows, width = slab.shape
    tile = 256
    f32 = jnp.float32
    vmem = pl.BlockSpec(memory_space=pltpu.VMEM)
    return pl.pallas_call(
        functools.partial(remainder_kernel, tile=tile),
        out_shape=(
            jax.ShapeDtypeStruct((rows, width), f32),
            jax.ShapeDtypeStruct(coupling.shape, f32),
            jax.ShapeDtypeStruct(turned.shape, f32),
        ),
        in_specs=[vmem] * 6,
        out_specs=(pl.BlockSpec(memory_space=pltpu.HBM),) * 3,
        scratch_shapes=[pltpu.VMEM((rows, width), f32), pltpu.SemaphoreType.DMA((rows // tile + 2,))],
        compiler_params=pltpu.CompilerParams(vmem_limit_bytes=16 << 20),
    )(whi, wlo, xrel, slab, coupling, turned)


def per_device(rows, planes, panels, slab):
    whi, wlo, xrel, coupling, turned = window(pltpu.with_memory_space_constraint(panels.T, pltpu.HBM), pltpu.with_memory_space_constraint(slab, pltpu.HBM), rows, planes)
    remainder, coupling, turned = remove(whi, wlo, xrel, slab, coupling, turned)
    return (turned.T, coupling, remainder)


def solution(mesh):
    placed = (P("prow", "pcol"), P("prow", "pcol"))
    return jax.shard_map(
        functools.partial(per_device, mesh.shape["prow"], mesh.shape["pcol"]),
        mesh=mesh,
        in_specs=placed,
        out_specs=(P(None, "pcol"), P(None, "pcol"), P("prow", "pcol")),
        check_vma=False,
    )
```
